32 devices in a mesh: row: 8 (over z, x), col: 4 (over y, core).
Axes of the slice: x: 2, y: 2, z: 4, core: 2. Of those that a mesh axis runs over, the one named last changes fastest.
Arguments:
- hamiltonian: float32 [18432, 18432], P('row', 'col'), may hold values from -6 to 6, as said below
- panel: float32 [18432, 128], P(('row', 'col')), may hold values from -0.03125 to 0.03125
Outputs:
- updated: float32 [18432, 18432], P('row', 'col')
The draws below stay inside these ranges and needn't reach their ends.
Inputs may be any that keep to these rules, and one draw needn't show every extreme that they name: `hamiltonian`: H is symmetric: the entry at stored row p and stored column q equals the entry whose stored row and column stand for the two global indices swapped.
All inputs are finite; a program needn't handle non-finite values.
Results may differ from the reference program's by a relative error of at most 0.0002.
Values sent between devices are 32-bit elements; how exact they have to be, the bound alone decides.
No kernel may reach another device: no remote copies, remote signals or barrier semaphores. Data moves between devices by JAX's collectives and lax.ppermute only.
A program may use at most 192 MiB of HBM per device.

```python
import jax
import jax.numpy as jnp
from jax import lax

B = 128
N = 18432
N_ROW = 8
N_COL = 4


def stored_positions(count, groups, block_width):
    position = jnp.arange(count, dtype=jnp.int32)
    per_group = count // groups
    group_index = position // per_group
    inside = position % per_group
    return (inside // block_width * groups + group_index) * block_width + inside % block_width


def draw_hamiltonian(key, part):
    sampled = jax.random.truncated_normal(key, -4.0, 4.0, (N, N), jnp.float32)
    symmetric = (sampled + sampled.T) * 0.5 ** 0.5
    row_order = stored_positions(N, N_ROW, B)
    col_order = stored_positions(N, N_COL, B)
    return jnp.take(jnp.take(symmetric, row_order, axis=0), col_order, axis=1)


def shard_levels(key, extent, split, smallest, top_value):
    def one(axis_at, blocks):
        draws = jax.random.uniform(jax.random.fold_in(jax.random.fold_in(key, 6), axis_at), (blocks,), jnp.float32, smallest / len(split), top_value / len(split))
        return jnp.repeat(jnp.exp(draws), extent[axis_at] // blocks).reshape((-1,) + (1,) * (len(extent) - axis_at - 1))

    loudness = one(*split[0])
    for cut in split[1:]:
        loudness = loudness * one(*cut)
    return loudness


def centred(stream_key, extent, spread, reach, cuts=(), held_as=jnp.bfloat16):
    gain = shard_levels(stream_key, extent, cuts, -0.22, 0.18) if cuts else 1.0
    values = jax.random.normal(stream_key, extent, jnp.float32) * spread * gain
    return jnp.minimum(jnp.maximum(values, -reach), reach).astype(held_as)


def setup_inputs(seed: int = 0) -> dict:
    seeds = jax.random.split(jax.random.key(seed), 3)
    hamiltonian = draw_hamiltonian(jax.random.fold_in(seeds[2], 71), 0)
    panel = centred(seeds[1], (N, B), (2 * N) ** -0.5, 0.03125, ((0, 32),), jnp.float32)
    return dict(hamiltonian=hamiltonian, panel=panel)


highest = lax.Precision.HIGHEST


def matmul(left, right):
    return jnp.dot(left, right, precision=highest, preferred_element_type=jnp.float32)


def stored_global(count, groups, block_width):
    position = jnp.arange(count, dtype=jnp.int32)
    per_group = count // groups
    group_index = position // per_group
    inside = position % per_group
    return ((inside // block_width) * groups + group_index) * block_width + inside % block_width


def shape_panel(panel_raw, global_rows, block_width):
    global_block = global_rows // block_width
    within = global_rows % block_width
    column_ids = jnp.arange(panel_raw.shape[1], dtype=jnp.int32)
    below = column_ids[None, :] < within[:, None]
    on_diagonal = column_ids[None, :] == within[:, None]
    unit_block = jnp.where(below, panel_raw, jnp.where(on_diagonal, 1.0, 0.0))
    kept = jnp.where((global_block == 1)[:, None], unit_block, 0.0)
    return jnp.where((global_block >= 2)[:, None], panel_raw, kept).astype(jnp.float32)


def upper_inverse(gram_matrix):
    width = gram_matrix.shape[0]
    diagonal_half = jnp.diag(gram_matrix) * 0.5
    nilpotent = jnp.triu(gram_matrix, 1) / diagonal_half[:, None]
    identity_matrix = jnp.eye(width, dtype=gram_matrix.dtype)
    power = -nilpotent
    result = identity_matrix + power
    for level in range(width.bit_length()):
        power = matmul(power, power)
        result = matmul(result, identity_matrix + power)
    return result / diagonal_half[None, :]


def compact_factors(gram_matrix, cross_term):
    block_factor = upper_inverse(gram_matrix)
    middle = matmul(matmul(block_factor.T, cross_term), block_factor)
    return block_factor, middle


def reference(hamiltonian, panel):
    row_map = stored_global(N, N_ROW, B)
    col_map = stored_global(N, N_COL, B)
    v_rows = shape_panel(panel, row_map, B)
    inverse_rows = jnp.zeros((N,), jnp.int32).at[row_map].set(jnp.arange(N, dtype=jnp.int32))
    v_cols = jnp.take(v_rows, inverse_rows[col_map], axis=0)
    p_rows = matmul(hamiltonian, v_cols)
    gram_matrix = matmul(v_rows.T, v_rows)
    cross_term = matmul(v_rows.T, p_rows)
    block_factor, middle = compact_factors(gram_matrix, cross_term)
    y_rows = matmul(p_rows, block_factor) - 0.5 * matmul(v_rows, middle)
    p_cols = lax.dot_general(hamiltonian, v_rows, (((0,), (0,)), ((), ())), precision=highest, preferred_element_type=jnp.float32)
    y_cols = matmul(p_cols, block_factor) - 0.5 * matmul(v_cols, middle)
    left_side = jnp.concatenate([v_rows, y_rows], axis=1)
    right_side = jnp.concatenate([y_cols, v_cols], axis=1)
    updated = hamiltonian - lax.dot_general(left_side, right_side, (((1,), (1,)), ((), ())), precision=highest, preferred_element_type=jnp.float32)
    return updated
```

```python
import functools

import jax
import jax.numpy as jnp
from jax import lax
from jax.experimental import pallas as pl
from jax.experimental.pallas import tpu as pltpu
from jax.sharding import PartitionSpec as P

B = 128
BOTH = ("row", "col")
HIGHEST = lax.Precision.HIGHEST
NT = (((1,), (1,)), ((), ()))


def matmul(left, right):
    return jnp.dot(left, right, precision=HIGHEST, preferred_element_type=jnp.float32)


def shape_panel(panel_raw, global_rows, block_width):
    global_block = (global_rows // block_width)[:, None]
    within = (global_rows % block_width)[:, None]
    column_ids = jnp.arange(panel_raw.shape[1], dtype=jnp.int32)[None, :]
    unit_block = jnp.where(
        column_ids < within, panel_raw, jnp.where(column_ids == within, 1.0, 0.0)
    )
    kept = jnp.where(global_block == 1, unit_block, 0.0)
    return jnp.where(global_block >= 2, panel_raw, kept)


def upper_inverse(gram_matrix):
    width = gram_matrix.shape[0]
    identity_matrix = jnp.eye(width, dtype=gram_matrix.dtype)
    diagonal_half = jnp.sum(gram_matrix * identity_matrix, axis=1) * 0.5
    nilpotent = jnp.triu(gram_matrix, 1) / diagonal_half[:, None]
    power = -nilpotent
    result = identity_matrix + power
    for level in range(width.bit_length()):
        power = matmul(power, power)
        result = matmul(result, identity_matrix + power)
    diagonal_row = jnp.sum(gram_matrix * identity_matrix, axis=0) * 0.5
    return result / diagonal_row[None, :]


def halves(x):
    high = x.astype(jnp.bfloat16)
    low = (x - high.astype(jnp.float32)).astype(jnp.bfloat16)
    return high, low


def beside(*arrays):
    return jnp.concatenate(arrays, axis=1)


def group_of(blocks):
    return next(g for g in (3, 2, 1) if blocks % g == 0)


def product_kernel(groups, width, per_step, h_ref, v_ref, out_ref, total):
    step = pl.program_id(0)

    @pl.when(step == 0)
    def _():
        total[...] = jnp.zeros_like(total)

    parts = []
    for i in range(per_step):
        for s in range(groups):
            parts.append(beside(*halves(v_ref[s, i * width : (i + 1) * width, :])))
    right = jnp.concatenate(parts, axis=0)
    high, low = halves(h_ref[...])
    total[...] += jnp.dot(
        high, right, preferred_element_type=jnp.float32
    ) + jnp.dot(low, right, preferred_element_type=jnp.float32)

    @pl.when(step == pl.num_programs(0) - 1)
    def _():
        out_ref[...] = total[:, :width] + total[:, width:]


def product(h, v):
    rows, columns = h.shape
    groups, group_rows, width = v.shape
    per_step = group_of(group_rows // width)
    tile = groups * per_step * width
    return pl.pallas_call(
        functools.partial(product_kernel, groups, width, per_step),
        out_shape=jax.ShapeDtypeStruct((rows, width), jnp.float32),
        grid=(columns // tile,),
        in_specs=[
            pl.BlockSpec((rows, tile), lambda k: (0, k)),
            pl.BlockSpec((groups, per_step * width, width), lambda k: (0, k, 0)),
        ],
        out_specs=pl.BlockSpec((rows, width), lambda k: (0, 0)),
        scratch_shapes=[pltpu.VMEM((rows, 2 * width), jnp.float32)],
        compiler_params=pltpu.CompilerParams(
            dimension_semantics=("arbitrary",), vmem_limit_bytes=48 << 20
        ),
        cost_estimate=pl.CostEstimate(
            flops=8 * rows * columns * width,
            bytes_accessed=4 * rows * columns,
            transcendentals=0,
        ),
        name="panel_product",
    )(h, v)


def update_kernel(
    groups, width, per_step, h_ref, vr_ref, pr_ref, vc_ref, pc_ref, mix_ref, out_ref, left, mix
):
    step = pl.program_id(0)

    def y_of(p, v):
        p_high, p_low = halves(p)
        v_high, v_low = halves(v)
        y = jnp.dot(
            beside(p_high, v_high, p_high, v_high, p_low, v_low),
            mix[...],
            preferred_element_type=jnp.float32,
        )
        return halves(y), (v_high, v_low)

    @pl.when(step == 0)
    def _():
        high, low = halves(mix_ref[...])
        size = high.shape[0]
        mix[:size] = high
        mix[size : 2 * size] = low
        mix[2 * size :] = high
        for r in range(0, h_ref.shape[0], width):
            at = slice(r, r + width)
            (y_high, y_low), (v_high, v_low) = y_of(pr_ref[at, :], vr_ref[at, :])
            left[at, :] = beside(v_high, y_high, v_high, y_high, v_low, y_low)

    parts = []
    for i in range(per_step):
        for s in range(groups):
            at = slice(i * width, (i + 1) * width)
            (y_high, y_low), (v_high, v_low) = y_of(pc_ref[s, at, :], vc_ref[s, at, :])
            parts.append(beside(y_high, v_high, y_low, v_low, y_high, v_high))
    right = jnp.concatenate(parts, axis=0)
    out_ref[...] = h_ref[...] - lax.dot_general(
        left[...], right, NT, preferred_element_type=jnp.float32
    )


def update(h, v_rows, p_rows, v_cols, p_cols, mix):
    rows, columns = h.shape
    groups, group_rows, width = v_cols.shape
    per_step = group_of(group_rows // width)
    tile = groups * per_step * width
    whole = lambda shape: pl.BlockSpec(
        shape, lambda k: (0,) * len(shape), pipeline_mode=pl.Buffered(1)
    )
    piece = pl.BlockSpec((groups, per_step * width, width), lambda k: (0, k, 0))
    return pl.pallas_call(
        functools.partial(update_kernel, groups, width, per_step),
        out_shape=jax.ShapeDtypeStruct(h.shape, jnp.float32),
        grid=(columns // tile,),
        in_specs=[
            pl.BlockSpec((rows, tile), lambda k: (0, k)),
            whole((rows, width)),
            whole((rows, width)),
            piece,
            piece,
            whole((2 * width, width)),
        ],
        out_specs=pl.BlockSpec((rows, tile), lambda k: (0, k)),
        scratch_shapes=[
            pltpu.VMEM((rows, 6 * width), jnp.bfloat16),
            pltpu.VMEM((6 * width, width), jnp.bfloat16),
        ],
        compiler_params=pltpu.CompilerParams(
            dimension_semantics=("arbitrary",), vmem_limit_bytes=52 << 20
        ),
        cost_estimate=pl.CostEstimate(
            flops=12 * rows * columns * width,
            bytes_accessed=8 * rows * columns,
            transcendentals=0,
        ),
        name="rank_update",
    )(h, v_rows, p_rows, v_cols, p_cols, mix)


class Place:
    def __init__(self):
        self.rows = lax.axis_size("row")
        self.cols = lax.axis_size("col")
        self.row = lax.axis_index("row")
        self.col = lax.axis_index("col")
        self.pairs = self.cols // 2

    def to_shard(self, x, shift):
        route = []
        for g in range(self.rows):
            for c in range(self.cols):
                piece = (c // 2 + shift) % self.pairs * 2 + c % 2
                target = g // self.cols * self.cols + piece
                route.append((g * self.cols + c, target * self.cols + g % self.cols))
        return lax.ppermute(x, BOTH, route)

    def other_core(self, x):
        return lax.ppermute(x, "col", [(c, c ^ 1) for c in range(self.cols)])

    def along_pairs(self, x, shift):
        n = self.pairs
        return lax.ppermute(
            x, "col", [(c, (c // 2 + shift) % n * 2 + c % 2) for c in range(self.cols)]
        )

    def ring(self, x, shift):
        n = self.rows
        order = list(range(0, n, 2)) + list(range(1, n, 2))[::-1]
        return lax.ppermute(
            x, "row", [(order[i], order[(i + shift) % n]) for i in range(n)]
        )

    def ring_at(self, shift):
        n = self.rows
        r = self.row
        here = jnp.where(r % 2 == 0, r // 2, n - 1 - r // 2)
        there = (here - shift) % n
        return jnp.where(there < n // 2, 2 * there, 2 * (n - there) - 1)

    def gather_ring(self, shard):
        n = self.rows
        size = shard.shape[0]
        half = size // 16 * 8
        out = jnp.zeros((n,) + shard.shape, shard.dtype)

        def put(out, x, shift, start=0):
            return lax.dynamic_update_slice(out, x[None], (self.ring_at(shift), start, 0))

        out = put(out, shard, 0)
        ahead = back = shard
        for d in range(1, n // 2):
            ahead = self.ring(ahead, 1)
            back = self.ring(back, -1)
            out = put(put(out, ahead, d), back, -d)
        ahead = self.ring(ahead[:half], 1)
        back = self.ring(back[half:], -1)
        out = put(out, ahead, n // 2)
        return put(out, back, n // 2, half)

    def gather_col(self, piece):
        out = jnp.zeros((self.cols,) + piece.shape, piece.dtype)
        hi, core = self.col // 2, self.col % 2

        def put(out, x, at):
            return lax.dynamic_update_slice(out, x[None], (at, 0, 0))

        for d in range(self.pairs):
            mine = piece if d == 0 else self.along_pairs(piece, d)
            at = (hi - d) % self.pairs * 2
            out = put(out, mine, at + core)
            out = put(out, self.other_core(mine), at + 1 - core)
        return out.reshape(-1, piece.shape[1])

    def sum_all(self, x):
        for axis, size in (("col", self.cols), ("row", self.rows)):
            bit = 1
            while bit < size:
                x = x + lax.ppermute(x, axis, [(i, i ^ bit) for i in range(size)])
                bit *= 2
        return x

    def scatter_sum(self, partial):
        hi, core = self.col // 2, self.col % 2
        width = partial.shape[1]
        pieces = partial.reshape(self.pairs, 2, -1, width)
        pick = lambda k: lax.dynamic_index_in_dim(pieces, k, 1, keepdims=False)
        mine = pick(core) + self.other_core(pick(1 - core))
        at = lambda d: lax.dynamic_index_in_dim(
            mine, (hi + d) % self.pairs, 0, keepdims=False
        )
        shard = self.to_shard(at(0), 0)
        own = at(0)
        for d in range(1, self.pairs):
            shard = shard + self.to_shard(at(d), d)
            own = own + self.along_pairs(at(d), d)
        return own, shard


def body(hamiltonian, panel):
    place = Place()
    width = panel.shape[1]
    piece_rows = panel.shape[0]
    groups = place.rows // place.cols
    position = place.col * piece_rows + jnp.arange(piece_rows, dtype=jnp.int32)
    global_rows = (position // B * place.rows + place.row) * B + position % B
    piece = shape_panel(panel, global_rows, B)

    shard = place.to_shard(piece, 0)
    v_cols = place.gather_ring(shard).reshape(groups, -1, width)
    v_rows = place.gather_col(piece)
    gram_matrix = place.sum_all(matmul(piece.T, piece))
    block_factor = upper_inverse(gram_matrix)

    partial = product(hamiltonian, v_cols)
    cross_term = place.sum_all(matmul(v_rows.T, partial))
    own, shard = place.scatter_sum(partial)
    p_cols = place.gather_ring(shard).reshape(groups, -1, width)
    p_rows = place.gather_col(own)
    middle = matmul(matmul(block_factor.T, cross_term), block_factor)
    mix = jnp.concatenate([block_factor, -0.5 * middle], axis=0)
    return update(hamiltonian, v_rows, p_rows, v_cols, p_cols, mix)


def solution(mesh):
    return jax.shard_map(
        body,
        mesh=mesh,
        in_specs=(P("row", "col"), P(("row", "col"), None)),
        out_specs=P("row", "col"),
        check_vma=False,
    )
```

```python
import functools

import jax
import jax.numpy as jnp
from jax import lax
from jax.experimental import pallas as pl
from jax.experimental.pallas import tpu as pltpu
from jax.sharding import PartitionSpec as P


B = 128
BOTH = ("row", "col")
HIGHEST = lax.Precision.HIGHEST
NT = (((1,), (1,)), ((), ()))


def matmul(left, right):
    return jnp.dot(left, right, precision=HIGHEST, preferred_element_type=jnp.float32)


def shape_panel(panel_raw, global_rows, block_width):
    global_block = (global_rows // block_width)[:, None]
    within = (global_rows % block_width)[:, None]
    column_ids = jnp.arange(panel_raw.shape[1], dtype=jnp.int32)[None, :]
    unit_block = jnp.where(
        column_ids < within, panel_raw, jnp.where(column_ids == within, 1.0, 0.0)
    )
    kept = jnp.where(global_block == 1, unit_block, 0.0)
    return jnp.where(global_block >= 2, panel_raw, kept)


def upper_inverse(gram_matrix):
    width = gram_matrix.shape[0]
    identity_matrix = jnp.eye(width, dtype=gram_matrix.dtype)
    diagonal_half = jnp.sum(gram_matrix * identity_matrix, axis=1) * 0.5
    nilpotent = jnp.triu(gram_matrix, 1) / diagonal_half[:, None]
    power = -nilpotent
    result = identity_matrix + power
    for _ in range(width.bit_length()):
        power = matmul(power, power)
        result = matmul(result, identity_matrix + power)
    diagonal_row = jnp.sum(gram_matrix * identity_matrix, axis=0) * 0.5
    return result / diagonal_row[None, :]


def halves(x):
    high = x.astype(jnp.bfloat16)
    low = (x - high.astype(jnp.float32)).astype(jnp.bfloat16)
    return high, low


def beside(*arrays):
    return jnp.concatenate(arrays, axis=1)


def group_of(blocks, sizes):
    return next(g for g in sizes if blocks % g == 0)


def in_vmem(x):
    return pltpu.with_memory_space_constraint(x, pltpu.VMEM)


def product_kernel(
    groups, width, per_step, cols, here_ref, h_ref, v_ref, kept_ref, own_ref, other_ref, gram_ref,
    total, inner, sems,
):
    step, steps = pl.program_id(0), pl.num_programs(0)
    tile = groups * width * per_step
    ahead = min(2, sems.shape[0])

    def copy(k):
        at = pl.ds(pl.multiple_of(k * tile, tile), tile)
        return pltpu.make_async_copy(h_ref.at[:, at], kept_ref.at[:, at], sems.at[k])

    @pl.when(step == 0)
    def _():
        for k in range(ahead):
            copy(k).start()
        total[...] = jnp.zeros_like(total)
        inner[...] = jnp.zeros_like(inner)

    parts = []
    for i in range(per_step):
        for s in range(groups):
            parts.append(beside(*halves(v_ref[s, i * width : (i + 1) * width, :])))
    right = jnp.concatenate(parts, axis=0)
    inner[...] += lax.dot_general(
        right, right, (((0,), (0,)), ((), ())), preferred_element_type=jnp.float32
    )

    @pl.when(step + ahead < steps)
    def _():
        copy(step + ahead).start()

    copy(step).wait()
    high, low = halves(kept_ref[:, pl.ds(pl.multiple_of(step * tile, tile), tile)])
    total[...] += jnp.dot(
        high, right, preferred_element_type=jnp.float32
    ) + jnp.dot(low, right, preferred_element_type=jnp.float32)

    @pl.when(step == steps - 1)
    def _():
        half = inner[:, :width] + inner[:, width:]
        gram_ref[...] = half[:width] + half[width:]
        size = own_ref.shape[1]
        pairs = cols // 2
        hi, core = here_ref[0], here_ref[1]
        for k in range(pairs):
            at = (k + pairs - hi) % pairs
            for c in range(2):
                rows = slice((2 * k + c) * size, (2 * k + c + 1) * size)
                value = total[rows, :width] + total[rows, width:]

                @pl.when(core == c)
                def _():
                    own_ref[at] = value

                @pl.when(core != c)
                def _():
                    other_ref[at] = value


def product(h, v, cols, here):
    rows, columns = h.shape
    groups, group_rows, width = v.shape
    per_step = group_of(group_rows // width, (3, 2, 1))
    tile = groups * per_step * width
    half = (cols // 2, rows // cols, width)
    steps = columns // tile
    return pl.pallas_call(
        functools.partial(product_kernel, groups, width, per_step, cols),
        out_shape=[
            pltpu.VMEM(h.shape, h.dtype),
            jax.ShapeDtypeStruct(half, jnp.float32),
            jax.ShapeDtypeStruct(half, jnp.float32),
            jax.ShapeDtypeStruct((width, width), jnp.float32),
        ],
        grid=(steps,),
        in_specs=[
            pl.BlockSpec(memory_space=pltpu.SMEM),
            pl.BlockSpec(memory_space=pl.ANY),
            pl.BlockSpec((groups, per_step * width, width), lambda k: (0, k, 0)),
        ],
        out_specs=[
            pl.BlockSpec(memory_space=pltpu.VMEM),
            pl.BlockSpec(half, lambda k: (0, 0, 0)),
            pl.BlockSpec(half, lambda k: (0, 0, 0)),
            pl.BlockSpec((width, width), lambda k: (0, 0)),
        ],
        scratch_shapes=[
            pltpu.VMEM((rows, 2 * width), jnp.float32),
            pltpu.VMEM((2 * width, 2 * width), jnp.float32),
            pltpu.SemaphoreType.DMA((steps,)),
        ],
        compiler_params=pltpu.CompilerParams(
            dimension_semantics=("arbitrary",), vmem_limit_bytes=20 << 20
        ),
        cost_estimate=pl.CostEstimate(
            flops=8 * rows * columns * width,
            bytes_accessed=4 * rows * columns,
            transcendentals=0,
        ),
        name="panel_product",
    )(here, h, v)


def update_kernel(
    groups, width, per_step, parts, *refs
):
    h_refs = refs[:parts]
    vr_ref, pr_ref, vc_ref, pc_ref, mix_ref, out_ref, left, mix = refs[parts:]
    step = pl.program_id(0)

    def y_of(p, v):
        p_high, p_low = halves(p)
        v_high, v_low = halves(v)
        y = jnp.dot(
            beside(p_high, v_high, p_high, v_high, p_low, v_low),
            mix[...],
            preferred_element_type=jnp.float32,
        )
        return halves(y), (v_high, v_low)

    @pl.when(step == 0)
    def _():
        high, low = halves(mix_ref[...])
        size = high.shape[0]
        mix[:size] = high
        mix[size : 2 * size] = low
        mix[2 * size :] = high
        for r in range(0, out_ref.shape[0], width):
            at = slice(r, r + width)
            (y_high, y_low), (v_high, v_low) = y_of(pr_ref[at, :], vr_ref[at, :])
            left[at, :] = beside(v_high, y_high, v_high, y_high, v_low, y_low)

    parts = []
    for i in range(per_step):
        for s in range(groups):
            at = slice(i * width, (i + 1) * width)
            (y_high, y_low), (v_high, v_low) = y_of(pc_ref[s, at, :], vc_ref[s, at, :])
            parts.append(beside(y_high, v_high, y_low, v_low, y_high, v_high))
    right = jnp.concatenate(parts, axis=0)
    tile = out_ref.shape[1]
    at = pl.ds(pl.multiple_of(step * tile, tile), tile)
    size = out_ref.shape[0] // 2
    for k in range(2):
        rows = slice(k * size, (k + 1) * size)
        out_ref[rows, :] = h_refs[0][rows, at] - lax.dot_general(
            left[rows, :], right, NT, preferred_element_type=jnp.float32
        )


def update(held, v_rows, p_rows, v_cols, p_cols, mix):
    rows, columns = sum(h.shape[0] for h in held), held[0].shape[1]
    groups, group_rows, width = v_cols.shape
    per_step = group_of(group_rows // width, (2, 3, 1))
    tile = groups * per_step * width
    whole = lambda shape: pl.BlockSpec(
        shape, lambda k: (0,) * len(shape), pipeline_mode=pl.Buffered(1)
    )
    piece = pl.BlockSpec((groups, per_step * width, width), lambda k: (0, k, 0))
    return pl.pallas_call(
        functools.partial(update_kernel, groups, width, per_step, len(held)),
        out_shape=jax.ShapeDtypeStruct((rows, columns), jnp.float32),
        grid=(columns // tile,),
        in_specs=[
            *[pl.BlockSpec(memory_space=pltpu.VMEM)] * len(held),
            whole((rows, width)),
            whole((rows, width)),
            piece,
            piece,
            whole((2 * width, width)),
        ],
        out_specs=pl.BlockSpec((rows, tile), lambda k: (0, k)),
        scratch_shapes=[
            pltpu.VMEM((rows, 6 * width), jnp.bfloat16),
            pltpu.VMEM((6 * width, width), jnp.bfloat16),
        ],
        compiler_params=pltpu.CompilerParams(
            dimension_semantics=("arbitrary",), vmem_limit_bytes=20 << 20
        ),
        cost_estimate=pl.CostEstimate(
            flops=12 * rows * columns * width,
            bytes_accessed=8 * rows * columns,
            transcendentals=0,
        ),
        name="rank_update",
    )(*map(in_vmem, held), v_rows, p_rows, v_cols, p_cols, mix)


class Place:
    def __init__(self):
        self.rows = lax.axis_size("row")
        self.cols = lax.axis_size("col")
        self.row = lax.axis_index("row")
        self.col = lax.axis_index("col")
        self.pairs = self.cols // 2
        n = self.rows
        self.places = {d: self.ring_at(d) for d in range(-(n // 2), n // 2 + 1)}
        hi, core = self.col // 2, self.col % 2
        self.same_core = [(hi - d) % self.pairs * 2 + core for d in range(self.pairs)]
        self.other = [(hi - d) % self.pairs * 2 + 1 - core for d in range(self.pairs)]
        self.here = jnp.stack([hi, core]).astype(jnp.int32)

    def before(self, x):
        known = (self.places, self.same_core, self.other, self.here)
        known, x = lax.optimization_barrier((known, x))
        self.places, self.same_core, self.other, self.here = known
        return x

    def to_shard(self, x, shift):
        route = []
        for g in range(self.rows):
            for c in range(self.cols):
                piece = (c // 2 + shift) % self.pairs * 2 + c % 2
                target = g // self.cols * self.cols + piece
                route.append((g * self.cols + c, target * self.cols + g % self.cols))
        return lax.ppermute(x, BOTH, route)

    def other_core(self, x):
        return lax.ppermute(x, "col", [(c, c ^ 1) for c in range(self.cols)])

    def along_pairs(self, x, shift):
        n = self.pairs
        return lax.ppermute(
            x, "col", [(c, (c // 2 + shift) % n * 2 + c % 2) for c in range(self.cols)]
        )

    def ring(self, x, shift):
        n = self.rows
        order = list(range(0, n, 2)) + list(range(1, n, 2))[::-1]
        return lax.ppermute(
            x, "row", [(order[i], order[(i + shift) % n]) for i in range(n)]
        )

    def ring_at(self, shift):
        n = self.rows
        r = self.row
        here = jnp.where(r % 2 == 0, r // 2, n - 1 - r // 2)
        there = (here - shift) % n
        return jnp.where(there < n // 2, 2 * there, 2 * (n - there) - 1)

    def gather_ring(self, shard, asides=(), held=None):
        n = self.rows
        half = shard.shape[0] // 16 * 8
        asides = list(asides) + [lambda seen: None] * n
        held = {} if held is None else held
        held[0] = ahead = back = shard
        for d in range(1, n // 2 + 1):
            if d == n // 2:
                ahead, back = ahead[:half], back[half:]
            seen = ahead
            held[d] = ahead = self.ring(ahead, 1)
            held[-d] = back = self.ring(back, -1)
            asides[d - 1](seen)
        out = jnp.zeros((n,) + shard.shape, shard.dtype)
        for d, x in held.items():
            start = half if d == -(n // 2) else 0
            out = put(out, x, self.places[d], start)
        return out

    def sum_col(self, x):
        total = x
        for bit in range(1, self.cols):
            total = total + lax.ppermute(x, "col", [(c, c ^ bit) for c in range(self.cols)])
        return total

    def sum_bit(self, x, bit):
        n = self.rows
        return x + lax.ppermute(x, "row", [(r, r ^ bit) for r in range(n)])


def put(out, x, at, start=0):
    return lax.dynamic_update_slice(
        out, x[None], (at, start, 0), allow_negative_indices=False
    )


def after(x, seen):
    return lax.optimization_barrier((x, seen))[0]


class ColGather:
    def __init__(self, place, piece):
        self.place, self.piece = place, piece

    def first(self, seen):
        self.piece = after(self.piece, seen)
        self.mine = [self.piece] + [
            self.place.along_pairs(self.piece, d) for d in range(1, self.place.pairs)
        ]

    def second(self, seen):
        place = self.place
        self.mine = [after(x, seen) for x in self.mine]
        self.theirs = [place.other_core(x) for x in self.mine]

    def rows(self):
        place = self.place
        out = jnp.zeros((place.cols,) + self.piece.shape, self.piece.dtype)
        for d in range(place.pairs):
            out = put(out, self.mine[d], place.same_core[d])
            out = put(out, self.theirs[d], place.other[d])
        return out.reshape(-1, self.piece.shape[1])


def step(hamiltonian, panel):
    place = Place()
    width = panel.shape[1]
    piece_rows = panel.shape[0]
    groups = place.rows // place.cols
    position = place.col * piece_rows + jnp.arange(piece_rows, dtype=jnp.int32)
    global_rows = (position // B * place.rows + place.row) * B + position % B
    piece = place.before(shape_panel(panel, global_rows, B))

    sums = {}

    def add_bit(name, bit):
        def run(seen):
            if bit < place.rows:
                sums[name] = place.sum_bit(after(sums[name], seen), bit)

        return run

    def both(*runs):
        def run(seen):
            for r in runs:
                r(seen)

        return run

    levels = place.rows.bit_length() - 1
    v_shard = place.to_shard(piece, 0)
    v_gather = ColGather(place, piece)
    v_cols = place.gather_ring(v_shard, (v_gather.first, lambda seen: None, v_gather.second))
    v_cols = v_cols.reshape(groups, -1, width)
    v_rows = v_gather.rows()
    kept, own, other, gram = product(hamiltonian, v_cols, place.cols, place.here)

    mine = own + place.other_core(other)
    p_shard = place.to_shard(mine[0], 0)
    for d in range(1, place.pairs):
        p_shard = p_shard + place.to_shard(mine[d], d)
    v_mine = [v_gather.mine[-d % place.pairs] for d in range(place.pairs)]
    cross = sum(matmul(v_mine[d].T, mine[d]) for d in range(place.pairs))
    sums["cross"] = place.sum_col(cross)
    gram = place.sum_col(after(gram, mine))
    block_factor = upper_inverse(gram)

    def own_piece(seen):
        own = mine[0]
        for d in range(1, place.pairs):
            own = own + place.along_pairs(after(mine[d], seen), d)
        sums["gather"] = ColGather(place, own)

    p_cols = place.gather_ring(
        p_shard,
        (
            both(add_bit("cross", 1), own_piece),
            both(add_bit("cross", 2), lambda seen: sums["gather"].first(seen)),
            both(add_bit("cross", 4), lambda seen: sums["gather"].second(seen)),
            *(add_bit("cross", 1 << k) for k in range(3, levels)),
        ),
    ).reshape(groups, -1, width)
    middle = matmul(matmul(block_factor.T, sums["cross"]), block_factor)
    mix = jnp.concatenate([block_factor, -0.5 * middle], axis=0)
    return update(
        [kept], v_rows, sums["gather"].rows(), v_cols, p_cols, mix
    )


def solution(mesh):
    return jax.shard_map(
        step,
        mesh=mesh,
        in_specs=(P("row", "col"), P(("row", "col"), None)),
        out_specs=P("row", "col"),
        check_vma=False,
    )
```

```python
import functools

import jax
import jax.numpy as jnp
from jax import lax
from jax.experimental import pallas as pl
from jax.experimental.pallas import tpu as pltpu
from jax.sharding import PartitionSpec as P


B = 128
BOTH = ("row", "col")
HIGHEST = lax.Precision.HIGHEST
NT = (((1,), (1,)), ((), ()))


def matmul(left, right):
    return jnp.dot(left, right, precision=HIGHEST, preferred_element_type=jnp.float32)


def shape_panel(panel_raw, global_rows, block_width):
    global_block = (global_rows // block_width)[:, None]
    within = (global_rows % block_width)[:, None]
    column_ids = jnp.arange(panel_raw.shape[1], dtype=jnp.int32)[None, :]
    unit_block = jnp.where(
        column_ids < within, panel_raw, jnp.where(column_ids == within, 1.0, 0.0)
    )
    kept = jnp.where(global_block == 1, unit_block, 0.0)
    return jnp.where(global_block >= 2, panel_raw, kept)


def upper_inverse(gram_matrix):
    width = gram_matrix.shape[0]
    identity_matrix = jnp.eye(width, dtype=gram_matrix.dtype)
    diagonal_half = jnp.sum(gram_matrix * identity_matrix, axis=1) * 0.5
    nilpotent = jnp.triu(gram_matrix, 1) / diagonal_half[:, None]
    power = -nilpotent
    result = identity_matrix + power
    for _ in range(width.bit_length()):
        power = matmul(power, power)
        result = matmul(result, identity_matrix + power)
    diagonal_row = jnp.sum(gram_matrix * identity_matrix, axis=0) * 0.5
    return result / diagonal_row[None, :]


def halves(x):
    high = x.astype(jnp.bfloat16)
    low = (x - high.astype(jnp.float32)).astype(jnp.bfloat16)
    return high, low


def beside(*arrays):
    return jnp.concatenate(arrays, axis=1)


def group_of(blocks, sizes):
    return next(g for g in sizes if blocks % g == 0)


def in_vmem(x):
    return pltpu.with_memory_space_constraint(x, pltpu.VMEM)


def product_kernel(
    groups, width, per_step, cols, here_ref, h_ref, v_ref, kept_ref, own_ref, other_ref, gram_ref,
    total, inner, sems,
):
    step, steps = pl.program_id(0), pl.num_programs(0)
    tile = groups * width * per_step
    ahead = min(2, sems.shape[0])

    def copy(k):
        at = pl.ds(pl.multiple_of(k * tile, tile), tile)
        return pltpu.make_async_copy(h_ref.at[:, at], kept_ref.at[:, at], sems.at[k])

    @pl.when(step == 0)
    def _():
        for k in range(ahead):
            copy(k).start()
        total[...] = jnp.zeros_like(total)
        inner[...] = jnp.zeros_like(inner)

    parts = []
    for i in range(per_step):
        for s in range(groups):
            parts.append(beside(*halves(v_ref[s, i * width : (i + 1) * width, :])))
    right = jnp.concatenate(parts, axis=0)
    inner[...] += lax.dot_general(
        right, right, (((0,), (0,)), ((), ())), preferred_element_type=jnp.float32
    )

    @pl.when(step + ahead < steps)
    def _():
        copy(step + ahead).start()

    copy(step).wait()
    high, low = halves(kept_ref[:, pl.ds(pl.multiple_of(step * tile, tile), tile)])
    total[...] += jnp.dot(
        high, right, preferred_element_type=jnp.float32
    ) + jnp.dot(low, right, preferred_element_type=jnp.float32)

    @pl.when(step == steps - 1)
    def _():
        half = inner[:, :width] + inner[:, width:]
        gram_ref[...] = half[:width] + half[width:]
        size = own_ref.shape[1]
        pairs = cols // 2
        hi, core = here_ref[0], here_ref[1]
        for k in range(pairs):
            at = (k + pairs - hi) % pairs
            for c in range(2):
                rows = slice((2 * k + c) * size, (2 * k + c + 1) * size)
                value = total[rows, :width] + total[rows, width:]

                @pl.when(core == c)
                def _():
                    own_ref[at] = value

                @pl.when(core != c)
                def _():
                    other_ref[at] = value


def product(h, v, cols, here):
    rows, columns = h.shape
    groups, group_rows, width = v.shape
    per_step = group_of(group_rows // width, (3, 2, 1))
    tile = groups * per_step * width
    half = (cols // 2, rows // cols, width)
    steps = columns // tile
    return pl.pallas_call(
        functools.partial(product_kernel, groups, width, per_step, cols),
        out_shape=[
            pltpu.VMEM(h.shape, h.dtype),
            jax.ShapeDtypeStruct(half, jnp.float32),
            jax.ShapeDtypeStruct(half, jnp.float32),
            jax.ShapeDtypeStruct((width, width), jnp.float32),
        ],
        grid=(steps,),
        in_specs=[
            pl.BlockSpec(memory_space=pltpu.SMEM),
            pl.BlockSpec(memory_space=pl.ANY),
            pl.BlockSpec((groups, per_step * width, width), lambda k: (0, k, 0)),
        ],
        out_specs=[
            pl.BlockSpec(memory_space=pltpu.VMEM),
            pl.BlockSpec(half, lambda k: (0, 0, 0)),
            pl.BlockSpec(half, lambda k: (0, 0, 0)),
            pl.BlockSpec((width, width), lambda k: (0, 0)),
        ],
        scratch_shapes=[
            pltpu.VMEM((rows, 2 * width), jnp.float32),
            pltpu.VMEM((2 * width, 2 * width), jnp.float32),
            pltpu.SemaphoreType.DMA((steps,)),
        ],
        compiler_params=pltpu.CompilerParams(
            dimension_semantics=("arbitrary",), vmem_limit_bytes=20 << 20
        ),
        cost_estimate=pl.CostEstimate(
            flops=8 * rows * columns * width,
            bytes_accessed=4 * rows * columns,
            transcendentals=0,
        ),
        name="panel_product",
    )(here, h, v)


def update_kernel(
    groups, width, per_step, parts, *refs
):
    h_refs = refs[:parts]
    vr_ref, pr_ref, vc_ref, pc_ref, mix_ref, out_ref, left, mix = refs[parts:]
    step = pl.program_id(0)

    def y_of(p, v):
        p_high, p_low = halves(p)
        v_high, v_low = halves(v)
        y = jnp.dot(
            beside(p_high, v_high, p_high, v_high, p_low, v_low),
            mix[...],
            preferred_element_type=jnp.float32,
        )
        return halves(y), (v_high, v_low)

    @pl.when(step == 0)
    def _():
        high, low = halves(mix_ref[...])
        size = high.shape[0]
        mix[:size] = high
        mix[size : 2 * size] = low
        mix[2 * size :] = high
        for r in range(0, out_ref.shape[0], width):
            at = slice(r, r + width)
            (y_high, y_low), (v_high, v_low) = y_of(pr_ref[at, :], vr_ref[at, :])
            left[at, :] = beside(v_high, y_high, v_high, y_high, v_low, y_low)

    parts = []
    for i in range(per_step):
        for s in range(groups):
            at = slice(i * width, (i + 1) * width)
            (y_high, y_low), (v_high, v_low) = y_of(pc_ref[s, at, :], vc_ref[s, at, :])
            parts.append(beside(y_high, v_high, y_low, v_low, y_high, v_high))
    right = jnp.concatenate(parts, axis=0)
    tile = out_ref.shape[1]
    at = pl.ds(pl.multiple_of(step * tile, tile), tile)
    size = out_ref.shape[0] // 4
    for k in range(4):
        rows = slice(k * size, (k + 1) * size)
        out_ref[rows, :] = h_refs[0][rows, at] - lax.dot_general(
            left[rows, :], right, NT, preferred_element_type=jnp.float32
        )


def update(held, v_rows, p_rows, v_cols, p_cols, mix):
    rows, columns = sum(h.shape[0] for h in held), held[0].shape[1]
    groups, group_rows, width = v_cols.shape
    per_step = group_of(group_rows // width, (2, 3, 1))
    tile = groups * per_step * width
    whole = lambda shape: pl.BlockSpec(
        shape, lambda k: (0,) * len(shape), pipeline_mode=pl.Buffered(1)
    )
    piece = pl.BlockSpec((groups, per_step * width, width), lambda k: (0, k, 0))
    return pl.pallas_call(
        functools.partial(update_kernel, groups, width, per_step, len(held)),
        out_shape=jax.ShapeDtypeStruct((rows, columns), jnp.float32),
        grid=(columns // tile,),
        in_specs=[
            *[pl.BlockSpec(memory_space=pltpu.VMEM)] * len(held),
            whole((rows, width)),
            whole((rows, width)),
            piece,
            piece,
            whole((2 * width, width)),
        ],
        out_specs=pl.BlockSpec((rows, tile), lambda k: (0, k)),
        scratch_shapes=[
            pltpu.VMEM((rows, 6 * width), jnp.bfloat16),
            pltpu.VMEM((6 * width, width), jnp.bfloat16),
        ],
        compiler_params=pltpu.CompilerParams(
            dimension_semantics=("arbitrary",), vmem_limit_bytes=18 << 20
        ),
        cost_estimate=pl.CostEstimate(
            flops=12 * rows * columns * width,
            bytes_accessed=8 * rows * columns,
            transcendentals=0,
        ),
        name="rank_update",
    )(*map(in_vmem, held), v_rows, p_rows, v_cols, p_cols, mix)


class Place:
    def __init__(self):
        self.rows = lax.axis_size("row")
        self.cols = lax.axis_size("col")
        self.row = lax.axis_index("row")
        self.col = lax.axis_index("col")
        self.pairs = self.cols // 2
        n = self.rows
        self.places = {d: self.ring_at(d) for d in range(-(n // 2), n // 2 + 1)}
        hi, core = self.col // 2, self.col % 2
        self.same_core = [(hi - d) % self.pairs * 2 + core for d in range(self.pairs)]
        self.other = [(hi - d) % self.pairs * 2 + 1 - core for d in range(self.pairs)]
        self.here = jnp.stack([hi, core]).astype(jnp.int32)

    def before(self, x):
        known = (self.places, self.same_core, self.other, self.here)
        known, x = lax.optimization_barrier((known, x))
        self.places, self.same_core, self.other, self.here = known
        return x

    def to_shard(self, x, shift):
        route = []
        for g in range(self.rows):
            for c in range(self.cols):
                piece = (c // 2 + shift) % self.pairs * 2 + c % 2
                target = g // self.cols * self.cols + piece
                route.append((g * self.cols + c, target * self.cols + g % self.cols))
        return lax.ppermute(x, BOTH, route)

    def other_core(self, x):
        return lax.ppermute(x, "col", [(c, c ^ 1) for c in range(self.cols)])

    def along_pairs(self, x, shift):
        n = self.pairs
        return lax.ppermute(
            x, "col", [(c, (c // 2 + shift) % n * 2 + c % 2) for c in range(self.cols)]
        )

    def ring(self, x, shift):
        n = self.rows
        order = list(range(0, n, 2)) + list(range(1, n, 2))[::-1]
        return lax.ppermute(
            x, "row", [(order[i], order[(i + shift) % n]) for i in range(n)]
        )

    def ring_at(self, shift):
        n = self.rows
        r = self.row
        here = jnp.where(r % 2 == 0, r // 2, n - 1 - r // 2)
        there = (here - shift) % n
        return jnp.where(there < n // 2, 2 * there, 2 * (n - there) - 1)

    def gather_ring(self, shard, asides=()):
        n = self.rows
        half = shard.shape[0] // 16 * 8
        asides = list(asides) + [lambda seen: None] * n
        held = [(shard, 0, 0)]
        ahead = back = (shard[:half], shard[half:])
        for d in range(1, n // 2 + 1):
            seen = ahead[0]
            if d < n // 2:
                moved = [(self.ring(a, 1), self.ring(b, -1)) for a, b in zip(ahead, back)]
                ahead, back = zip(*moved)
                for k, start in ((0, 0), (1, half)):
                    held += [(ahead[k], d, start), (back[k], -d, start)]
            else:
                held.append((self.ring(ahead[0], 1), d, 0))
                held.append((self.ring(back[1], -1), d, half))
            asides[d - 1](seen)
        out = jnp.zeros((n,) + shard.shape, shard.dtype)
        for x, d, start in held:
            out = put(out, x, self.places[d], start)
        return out

    def all_col(self, x):
        return [x] + [
            lax.ppermute(x, "col", [(c, c ^ bit) for c in range(self.cols)])
            for bit in range(1, self.cols)
        ]

    def other_bit(self, x, bit):
        n = self.rows
        return lax.ppermute(x, "row", [(r, r ^ bit) for r in range(n)])


def put(out, x, at, start=0):
    return lax.dynamic_update_slice(
        out, x[None], (at, start, 0), allow_negative_indices=False
    )


def after(x, seen):
    return lax.optimization_barrier((x, seen))[0]


class ColGather:
    def __init__(self, place, piece):
        self.place, self.piece = place, piece

    def first(self, seen):
        self.piece = after(self.piece, seen)
        self.mine = [self.piece] + [
            self.place.along_pairs(self.piece, d) for d in range(1, self.place.pairs)
        ]

    def second(self, seen):
        place = self.place
        self.mine = [after(x, seen) for x in self.mine]
        self.theirs = [place.other_core(x) for x in self.mine]

    def rows(self, seen=None):
        place = self.place
        if seen is not None:
            self.mine = [after(x, seen) for x in self.mine]
            self.theirs = [after(x, seen) for x in self.theirs]
        out = jnp.zeros((place.cols,) + self.piece.shape, self.piece.dtype)
        for d in range(place.pairs):
            out = put(out, self.mine[d], place.same_core[d])
            out = put(out, self.theirs[d], place.other[d])
        return out.reshape(-1, self.piece.shape[1])


def step(hamiltonian, panel):
    place = Place()
    width = panel.shape[1]
    piece_rows = panel.shape[0]
    groups = place.rows // place.cols
    position = place.col * piece_rows + jnp.arange(piece_rows, dtype=jnp.int32)
    global_rows = (position // B * place.rows + place.row) * B + position % B
    piece = place.before(shape_panel(panel, global_rows, B))

    sums = {}

    def add_bit(name, bit):
        def run(seen):
            if bit < place.rows:
                x = after(sum(sums[name]), seen)
                sums[name] = (x, place.other_bit(x, bit))

        return run

    def both(*runs):
        def run(seen):
            for r in runs:
                r(seen)

        return run

    v_shard = place.to_shard(piece, 0)
    v_gather = ColGather(place, piece)
    v_cols = place.gather_ring(v_shard, (v_gather.first, lambda seen: None, v_gather.second))
    v_cols = v_cols.reshape(groups, -1, width)
    kept, own, other, gram = product(hamiltonian, v_cols, place.cols, place.here)

    mine = own + place.other_core(other)
    p_shard = place.to_shard(mine[0], 0)
    for d in range(1, place.pairs):
        p_shard = p_shard + place.to_shard(mine[d], d)
    v_mine = [v_gather.mine[-d % place.pairs] for d in range(place.pairs)]
    cross = sum(matmul(v_mine[d].T, mine[d]) for d in range(place.pairs))
    grams = place.all_col(after(gram, mine))
    sums["cross"] = place.all_col(cross)
    block_factor = upper_inverse(sum(grams))

    def own_piece(seen):
        sums["own"] = [mine[0]] + [
            place.along_pairs(after(mine[d], seen), d) for d in range(1, place.pairs)
        ]

    def gather_first(seen):
        sums["gather"] = ColGather(place, sum(sums["own"]))
        sums["gather"].first(seen)
        sums["v_rows"] = v_gather.rows(seen)

    def skip(seen):
        return None

    def gather_second(seen):
        sums["gather"].second(seen)

    p_cols = place.gather_ring(
        p_shard,
        (
            both(add_bit("cross", 1), own_piece),
            both(add_bit("cross", 2), gather_first),
            add_bit("cross", 4),
            *(
                both(add_bit("cross", 1 << k), gather_second if k == 3 else skip)
                for k in range(3, place.rows // 2)
            ),
        ),
    ).reshape(groups, -1, width)
    middle = matmul(matmul(block_factor.T, sum(sums["cross"])), block_factor)
    mix = jnp.concatenate([block_factor, -0.5 * middle], axis=0)
    return update(
        [kept], sums["v_rows"], sums["gather"].rows(), v_cols, p_cols, mix
    )


def solution(mesh):
    return jax.shard_map(
        step,
        mesh=mesh,
        in_specs=(P("row", "col"), P(("row", "col"), None)),
        out_specs=P("row", "col"),
        check_vma=False,
    )
```

```python
import functools

import jax
import jax.numpy as jnp
from jax import lax
from jax.experimental import pallas as pl
from jax.experimental.pallas import tpu as pltpu
from jax.sharding import PartitionSpec as P


B = 128
BOTH = ("row", "col")
HIGHEST = lax.Precision.HIGHEST
NT = (((1,), (1,)), ((), ()))


def matmul(left, right):
    return jnp.dot(left, right, precision=HIGHEST, preferred_element_type=jnp.float32)


def shape_panel(panel_raw, global_rows, block_width):
    global_block = (global_rows // block_width)[:, None]
    within = (global_rows % block_width)[:, None]
    column_ids = jnp.arange(panel_raw.shape[1], dtype=jnp.int32)[None, :]
    unit_block = jnp.where(
        column_ids < within, panel_raw, jnp.where(column_ids == within, 1.0, 0.0)
    )
    kept = jnp.where(global_block == 1, unit_block, 0.0)
    return jnp.where(global_block >= 2, panel_raw, kept)


def upper_inverse(gram_matrix):
    width = gram_matrix.shape[0]
    identity_matrix = jnp.eye(width, dtype=gram_matrix.dtype)
    diagonal_half = jnp.sum(gram_matrix * identity_matrix, axis=1) * 0.5
    nilpotent = jnp.triu(gram_matrix, 1) / diagonal_half[:, None]
    power = -nilpotent
    result = identity_matrix + power
    for _ in range(width.bit_length()):
        power = matmul(power, power)
        result = matmul(result, identity_matrix + power)
    diagonal_row = jnp.sum(gram_matrix * identity_matrix, axis=0) * 0.5
    return result / diagonal_row[None, :]


def halves(x):
    high = x.astype(jnp.bfloat16)
    low = (x - high.astype(jnp.float32)).astype(jnp.bfloat16)
    return high, low


def beside(*arrays):
    return jnp.concatenate(arrays, axis=1)


def group_of(blocks, sizes):
    return next(g for g in sizes if blocks % g == 0)


def in_vmem(x):
    return pltpu.with_memory_space_constraint(x, pltpu.VMEM)


def product_kernel(
    groups, width, per_step, cols, here_ref, h_ref, v_ref, kept_ref, own_ref, other_ref, gram_ref,
    total, inner, sems,
):
    step, steps = pl.program_id(0), pl.num_programs(0)
    tile = groups * width * per_step
    ahead = min(2, sems.shape[0])

    def copy(k):
        at = pl.ds(pl.multiple_of(k * tile, tile), tile)
        return pltpu.make_async_copy(h_ref.at[:, at], kept_ref.at[:, at], sems.at[k])

    @pl.when(step == 0)
    def _():
        for k in range(ahead):
            copy(k).start()
        total[...] = jnp.zeros_like(total)
        inner[...] = jnp.zeros_like(inner)

    parts = []
    for i in range(per_step):
        for s in range(groups):
            parts.append(beside(*halves(v_ref[s, i * width : (i + 1) * width, :])))
    right = jnp.concatenate(parts, axis=0)
    inner[...] += lax.dot_general(
        right, right, (((0,), (0,)), ((), ())), preferred_element_type=jnp.float32
    )

    @pl.when(step + ahead < steps)
    def _():
        copy(step + ahead).start()

    copy(step).wait()
    high, low = halves(kept_ref[:, pl.ds(pl.multiple_of(step * tile, tile), tile)])
    total[...] += jnp.dot(
        high, right, preferred_element_type=jnp.float32
    ) + jnp.dot(low, right, preferred_element_type=jnp.float32)

    @pl.when(step == steps - 1)
    def _():
        half = inner[:, :width] + inner[:, width:]
        gram_ref[...] = half[:width] + half[width:]
        size = own_ref.shape[1]
        pairs = cols // 2
        hi, core = here_ref[0], here_ref[1]
        for k in range(pairs):
            at = (k + pairs - hi) % pairs
            for c in range(2):
                rows = slice((2 * k + c) * size, (2 * k + c + 1) * size)
                value = total[rows, :width] + total[rows, width:]

                @pl.when(core == c)
                def _():
                    own_ref[at] = value

                @pl.when(core != c)
                def _():
                    other_ref[at] = value


def product(h, v, cols, here):
    rows, columns = h.shape
    groups, group_rows, width = v.shape
    per_step = group_of(group_rows // width, (3, 2, 1))
    tile = groups * per_step * width
    half = (cols // 2, rows // cols, width)
    steps = columns // tile
    return pl.pallas_call(
        functools.partial(product_kernel, groups, width, per_step, cols),
        out_shape=[
            pltpu.VMEM(h.shape, h.dtype),
            jax.ShapeDtypeStruct(half, jnp.float32),
            jax.ShapeDtypeStruct(half, jnp.float32),
            jax.ShapeDtypeStruct((width, width), jnp.float32),
        ],
        grid=(steps,),
        in_specs=[
            pl.BlockSpec(memory_space=pltpu.SMEM),
            pl.BlockSpec(memory_space=pl.ANY),
            pl.BlockSpec((groups, per_step * width, width), lambda k: (0, k, 0)),
        ],
        out_specs=[
            pl.BlockSpec(memory_space=pltpu.VMEM),
            pl.BlockSpec(half, lambda k: (0, 0, 0)),
            pl.BlockSpec(half, lambda k: (0, 0, 0)),
            pl.BlockSpec((width, width), lambda k: (0, 0)),
        ],
        scratch_shapes=[
            pltpu.VMEM((rows, 2 * width), jnp.float32),
            pltpu.VMEM((2 * width, 2 * width), jnp.float32),
            pltpu.SemaphoreType.DMA((steps,)),
        ],
        compiler_params=pltpu.CompilerParams(
            dimension_semantics=("arbitrary",), vmem_limit_bytes=20 << 20
        ),
        cost_estimate=pl.CostEstimate(
            flops=8 * rows * columns * width,
            bytes_accessed=4 * rows * columns,
            transcendentals=0,
        ),
        name="panel_product",
    )(here, h, v)


def update_kernel(
    groups, width, per_step, parts, *refs
):
    h_refs = refs[:parts]
    vr_ref, pr_ref, vc_ref, pc_ref, mix_ref, out_ref, left, mix = refs[parts:]
    step = pl.program_id(0)

    def y_of(p, v):
        p_high, p_low = halves(p)
        v_high, v_low = halves(v)
        y = jnp.dot(
            beside(p_high, v_high, p_high, v_high, p_low, v_low),
            mix[...],
            preferred_element_type=jnp.float32,
        )
        return halves(y), (v_high, v_low)

    @pl.when(step == 0)
    def _():
        high, low = halves(mix_ref[...])
        size = high.shape[0]
        mix[:size] = high
        mix[size : 2 * size] = low
        mix[2 * size :] = high
        for r in range(0, out_ref.shape[0], width):
            at = slice(r, r + width)
            (y_high, y_low), (v_high, v_low) = y_of(pr_ref[at, :], vr_ref[at, :])
            left[at, :] = beside(v_high, y_high, v_high, y_high, v_low, y_low)

    parts = []
    for i in range(per_step):
        for s in range(groups):
            at = slice(i * width, (i + 1) * width)
            (y_high, y_low), (v_high, v_low) = y_of(pc_ref[s, at, :], vc_ref[s, at, :])
            parts.append(beside(y_high, v_high, y_low, v_low, y_high, v_high))
    right = jnp.concatenate(parts, axis=0)
    tile = out_ref.shape[1]
    at = pl.ds(pl.multiple_of(step * tile, tile), tile)
    size = out_ref.shape[0] // 4
    for k in range(4):
        rows = slice(k * size, (k + 1) * size)
        out_ref[rows, :] = h_refs[0][rows, at] - lax.dot_general(
            left[rows, :], right, NT, preferred_element_type=jnp.float32
        )


def update(held, v_rows, p_rows, v_cols, p_cols, mix):
    rows, columns = sum(h.shape[0] for h in held), held[0].shape[1]
    groups, group_rows, width = v_cols.shape
    per_step = group_of(group_rows // width, (2, 3, 1))
    tile = groups * per_step * width
    whole = lambda shape: pl.BlockSpec(
        shape, lambda k: (0,) * len(shape), pipeline_mode=pl.Buffered(1)
    )
    piece = pl.BlockSpec((groups, per_step * width, width), lambda k: (0, k, 0))
    return pl.pallas_call(
        functools.partial(update_kernel, groups, width, per_step, len(held)),
        out_shape=jax.ShapeDtypeStruct((rows, columns), jnp.float32),
        grid=(columns // tile,),
        in_specs=[
            *[pl.BlockSpec(memory_space=pltpu.VMEM)] * len(held),
            whole((rows, width)),
            whole((rows, width)),
            piece,
            piece,
            whole((2 * width, width)),
        ],
        out_specs=pl.BlockSpec((rows, tile), lambda k: (0, k)),
        scratch_shapes=[
            pltpu.VMEM((rows, 6 * width), jnp.bfloat16),
            pltpu.VMEM((6 * width, width), jnp.bfloat16),
        ],
        compiler_params=pltpu.CompilerParams(
            dimension_semantics=("arbitrary",), vmem_limit_bytes=18 << 20
        ),
        cost_estimate=pl.CostEstimate(
            flops=12 * rows * columns * width,
            bytes_accessed=8 * rows * columns,
            transcendentals=0,
        ),
        name="rank_update",
    )(*map(in_vmem, held), v_rows, p_rows, v_cols, p_cols, mix)


class Place:
    def __init__(self):
        self.rows = lax.axis_size("row")
        self.cols = lax.axis_size("col")
        self.row = lax.axis_index("row")
        self.col = lax.axis_index("col")
        self.pairs = self.cols // 2
        n = self.rows
        self.places = {d: self.ring_at(d) for d in range(-(n // 2), n // 2 + 1)}
        hi, core = self.col // 2, self.col % 2
        self.same_core = [(hi - d) % self.pairs * 2 + core for d in range(self.pairs)]
        self.other = [(hi - d) % self.pairs * 2 + 1 - core for d in range(self.pairs)]
        self.here = jnp.stack([hi, core]).astype(jnp.int32)

    def before(self, x):
        known = (self.places, self.same_core, self.other, self.here)
        known, x = lax.optimization_barrier((known, x))
        self.places, self.same_core, self.other, self.here = known
        return x

    def turned(self, j):
        return (self.pairs - 1 - j // 2) * 2 + j % 2

    def to_shard(self, x, shift):
        route = []
        for g in range(self.rows):
            for c in range(self.cols):
                piece = (c // 2 + shift) % self.pairs * 2 + c % 2
                target = g // self.cols * self.cols + self.turned(piece)
                route.append((g * self.cols + c, target * self.cols + g % self.cols))
        return lax.ppermute(x, BOTH, route)

    def other_core(self, x):
        return lax.ppermute(x, "col", [(c, c ^ 1) for c in range(self.cols)])

    def along_pairs(self, x, shift):
        n = self.pairs
        return lax.ppermute(
            x, "col", [(c, (c // 2 + shift) % n * 2 + c % 2) for c in range(self.cols)]
        )

    def ring(self, x, shift):
        n = self.rows
        order = list(range(0, n, 2)) + list(range(1, n, 2))[::-1]
        return lax.ppermute(
            x, "row", [(order[i], order[(i + shift) % n]) for i in range(n)]
        )

    def ring_at(self, shift):
        n = self.rows
        r = self.row
        here = jnp.where(r % 2 == 0, r // 2, n - 1 - r // 2)
        there = (here - shift) % n
        row = jnp.where(there < n // 2, 2 * there, 2 * (n - there) - 1)
        return row // self.cols * self.cols + self.turned(row % self.cols)

    def gather_ring(self, shard, asides=()):
        n = self.rows
        half = shard.shape[0] // 16 * 8
        asides = list(asides) + [lambda seen: None] * n
        held = [(shard, 0, 0)]
        ahead = back = (shard[:half], shard[half:])
        for d in range(1, n // 2 + 1):
            seen = ahead[0]
            if d < n // 2:
                moved = [(self.ring(a, 1), self.ring(b, -1)) for a, b in zip(ahead, back)]
                ahead, back = zip(*moved)
                for k, start in ((0, 0), (1, half)):
                    held += [(ahead[k], d, start), (back[k], -d, start)]
            else:
                held.append((self.ring(ahead[0], 1), d, 0))
                held.append((self.ring(back[1], -1), d, half))
            asides[d - 1](seen)
        out = jnp.zeros((n,) + shard.shape, shard.dtype)
        for x, d, start in held:
            out = put(out, x, self.places[d], start)
        return out

    def all_col(self, x):
        return [x] + [
            lax.ppermute(x, "col", [(c, c ^ bit) for c in range(self.cols)])
            for bit in range(1, self.cols)
        ]

    def other_bit(self, x, bit):
        n = self.rows
        return lax.ppermute(x, "row", [(r, r ^ bit) for r in range(n)])


def put(out, x, at, start=0):
    return lax.dynamic_update_slice(
        out, x[None], (at, start, 0), allow_negative_indices=False
    )


def after(x, seen):
    return lax.optimization_barrier((x, seen))[0]


class ColGather:
    def __init__(self, place, piece):
        self.place, self.piece = place, piece

    def first(self, seen):
        self.piece = after(self.piece, seen)
        self.mine = [self.piece] + [
            self.place.along_pairs(self.piece, d) for d in range(1, self.place.pairs)
        ]

    def second(self, seen):
        place = self.place
        self.mine = [after(x, seen) for x in self.mine]
        self.theirs = [place.other_core(x) for x in self.mine]

    def rows(self, seen=None):
        place = self.place
        if seen is not None:
            self.mine = [after(x, seen) for x in self.mine]
            self.theirs = [after(x, seen) for x in self.theirs]
        out = jnp.zeros((place.cols,) + self.piece.shape, self.piece.dtype)
        for d in range(place.pairs):
            out = put(out, self.mine[d], place.same_core[d])
            out = put(out, self.theirs[d], place.other[d])
        return out.reshape(-1, self.piece.shape[1])


def step(hamiltonian, panel):
    place = Place()
    width = panel.shape[1]
    piece_rows = panel.shape[0]
    groups = place.rows // place.cols
    position = place.col * piece_rows + jnp.arange(piece_rows, dtype=jnp.int32)
    global_rows = (position // B * place.rows + place.row) * B + position % B
    piece = shape_panel(panel, global_rows, B)
    hamiltonian = place.before(hamiltonian)

    sums = {}

    def add_bit(name, bit):
        def run(seen):
            if bit < place.rows:
                x = after(sum(sums[name]), seen)
                sums[name] = (x, place.other_bit(x, bit))

        return run

    def both(*runs):
        def run(seen):
            for r in runs:
                r(seen)

        return run

    v_shard = place.to_shard(piece, 0)
    v_gather = ColGather(place, piece)
    v_cols = place.gather_ring(v_shard, (v_gather.first, lambda seen: None, v_gather.second))
    v_cols = v_cols.reshape(groups, -1, width)
    kept, own, other, gram = product(hamiltonian, v_cols, place.cols, place.here)

    mine = own + place.other_core(other)
    p_shard = place.to_shard(mine[0], 0)
    for d in range(1, place.pairs):
        p_shard = p_shard + place.to_shard(mine[d], d)
    v_mine = [v_gather.mine[-d % place.pairs] for d in range(place.pairs)]
    cross = sum(matmul(v_mine[d].T, mine[d]) for d in range(place.pairs))
    grams = place.all_col(after(gram, mine))
    sums["cross"] = place.all_col(cross)
    block_factor = upper_inverse(sum(grams))

    def own_piece(seen):
        sums["own"] = [mine[0]] + [
            place.along_pairs(after(mine[d], seen), d) for d in range(1, place.pairs)
        ]

    def gather_first(seen):
        sums["gather"] = ColGather(place, sum(sums["own"]))
        sums["gather"].first(seen)
        sums["v_rows"] = v_gather.rows(seen)

    def skip(seen):
        return None

    def gather_second(seen):
        sums["gather"].second(seen)

    p_cols = place.gather_ring(
        p_shard,
        (
            both(add_bit("cross", 1), own_piece),
            both(add_bit("cross", 2), gather_first),
            add_bit("cross", 4),
            *(
                both(add_bit("cross", 1 << k), gather_second if k == 3 else skip)
                for k in range(3, place.rows // 2)
            ),
        ),
    ).reshape(groups, -1, width)
    middle = matmul(matmul(block_factor.T, sum(sums["cross"])), block_factor)
    mix = jnp.concatenate([block_factor, -0.5 * middle], axis=0)
    return update(
        [kept], sums["v_rows"], sums["gather"].rows(), v_cols, p_cols, mix
    )


def solution(mesh):
    return jax.shard_map(
        step,
        mesh=mesh,
        in_specs=(P("row", "col"), P(("row", "col"), None)),
        out_specs=P("row", "col"),
        check_vma=False,
    )
```
